512 devices in a mesh: space: 32 (over z_lo, x), tm: 16 (over y, z_hi, core).
Axes of the slice: x: 4, y: 4, z: 16 (z_hi: 2, z_lo: 8; z = z_hi * 8 + z_lo), core: 2. Of those that a mesh axis runs over, the one named last changes fastest.
Arguments:
- adjoint_end: float32 [16, 11, 128, 2048], P('tm', None, 'space'), may hold values from -6 to 6
- depth_fwd: float32 [16, 4, 128, 2048], P('tm', None, 'space'), may hold values from 0.3 to 2
- velocity_fwd: float32 [16, 4, 2, 128, 2048], P('tm', None, None, 'space'), may hold values from -3 to 3
- salt_fwd: bfloat16 [16, 4, 8, 128, 2048], P('tm', None, None, 'space'), may hold values from -6 to 6
- wet_mask: int32 [16, 128, 2048], P('tm', 'space'), may hold values 0 or 1
- cell_class: int32 [128, 2048], P('space'), may hold values 0 or 1
- manning: float32 [128, 2048], P('space'), may hold values from 0.02 to 0.1
- conductivity: float32 [8, 128, 2048], P(None, 'space'), may hold values from 0.01 to 1
Outputs:
- adjoint_start: float32 [16, 11, 128, 2048], P('tm', None, 'space')
- manning_grad: float32 [128, 2048], P('space', 'tm')
- cond_grad: float32 [8, 128, 2048], P(None, 'space', 'tm')
The draws below stay inside these ranges and needn't reach their ends.
Inputs may be any that keep to these rules, and one draw needn't show every extreme that they name: `wet_mask`: 1 marks a wet cell. `cell_class`: 1 marks a marsh cell, 0 a channel cell.
All inputs are finite; a program needn't handle non-finite values. No bound on the sum of `wet_mask` or of `cell_class` on one device may be relied on, other than what follows from the above.
Results may differ from the reference program's by a relative error of at most 0.0003.
Values sent between devices are 32-bit elements; how exact they have to be, the bound alone decides.
A program may use at most 64 MiB of HBM per device.

```python
import math
import jax
import jax.numpy as jnp
from jax import lax

NY = 2048
LAYERS = 8
STEPS = 4
NX = 128
WINDOWS = 16
FIELDS = 11


def with_ends(entries, rng, smallest, largest):
    longest = entries.shape.index(max(entries.shape))
    spots = []
    for shift in (0, 1):
        where = [jax.random.randint(jax.random.fold_in(rng, axis), (), 0, length) for axis, length in enumerate(entries.shape)]
        where[longest] = (where[longest] + shift) % entries.shape[longest]
        spots.append(tuple(where))
    return entries.at[spots[0]].set(smallest).at[spots[1]].set(largest)


def steps_of(key, dims, pieces, least, high):
    level, own = 1.0, jax.random.fold_in(key, 6)
    for axis_at, shards_of in pieces:
        draws = jnp.exp(jax.random.uniform(jax.random.fold_in(own, axis_at), (shards_of,), jnp.float32, least / len(pieces), high / len(pieces)))
        level = level * jnp.repeat(draws, dims[axis_at] // shards_of).reshape([-1 if axis == axis_at else 1 for axis in range(len(dims))])
    return level


def bell_draw(rng, dims, width, bound, shards=(), kind=jnp.bfloat16):
    array = jax.random.normal(rng, dims, jnp.float32) * width
    if len(shards) > 0:
        array = steps_of(rng, dims, shards, -0.22, 0.18) * array
    return jnp.clip(array, min=-bound, max=bound).astype(kind)


def setup_inputs(seed: int = 0) -> dict:
    key_of = jax.random.split(jax.random.key(seed), 9)
    return {
        "adjoint_end": bell_draw(key_of[0], (WINDOWS, FIELDS, NX, NY), 1.0, 6.0, ((0, 16), (2, 32)), jnp.float32),
        "depth_fwd": jnp.clip(jnp.exp(math.log(2.0) - 1.89712 * jax.random.uniform(key_of[1], (WINDOWS, STEPS, NX, NY), jnp.float32) ** steps_of(key_of[1], (WINDOWS, STEPS, NX, NY), ((0, 16), (2, 32)), -0.2, 0.2)), 0.3, 2.0),
        "velocity_fwd": bell_draw(key_of[2], (WINDOWS, STEPS, 2, NX, NY), 0.5, 3.0, ((0, 16), (3, 32)), jnp.float32),
        "salt_fwd": bell_draw(key_of[3], (WINDOWS, STEPS, LAYERS, NX, NY), 1.0, 6.0, ((0, 16), (3, 32))),
        "wet_mask": with_ends((jax.random.randint(key_of[4], (WINDOWS, NX, NY), 0, 5) < 4).astype(jnp.int32), jax.random.fold_in(key_of[4], 1), 0, 1),
        "cell_class": with_ends((jax.random.randint(key_of[5], (NX, NY), 0, 5) < 3).astype(jnp.int32), jax.random.fold_in(key_of[5], 1), 0, 1),
        "manning": jnp.clip(jnp.exp(math.log(0.1) - 1.609438 * jax.random.uniform(key_of[6], (NX, NY), jnp.float32) ** steps_of(key_of[6], (NX, NY), ((0, 32),), -0.2, 0.2)), 0.02, 0.1),
        "conductivity": jnp.clip(jnp.exp(math.log(1.0) - 4.6051702 * jax.random.uniform(key_of[7], (LAYERS, NX, NY), jnp.float32) ** steps_of(key_of[7], (LAYERS, NX, NY), ((1, 32),), -0.2, 0.2)), 0.01, 1.0),
    }


TIME_STEP = 0.4
GRAVITY = 9.81

def lower_diff(quantity, direction):
    length = quantity.shape[direction]
    head_rows = lax.slice_in_dim(quantity, 0, length - 1, axis=direction)
    zero_row = jnp.zeros_like(lax.slice_in_dim(quantity, 0, 1, axis=direction))
    return quantity - jnp.concatenate([zero_row, head_rows], axis=direction)

def upper_diff(quantity, direction):
    length = quantity.shape[direction]
    tail_rows = lax.slice_in_dim(quantity, 1, length, axis=direction)
    zero_row = jnp.zeros_like(lax.slice_in_dim(quantity, 0, 1, axis=direction))
    return jnp.concatenate([tail_rows, zero_row], axis=direction) - quantity

def friction(depth_now, velocity_now, manning):
    speed_now = jnp.sqrt(velocity_now[0] * velocity_now[0] + velocity_now[1] * velocity_now[1])
    powered = jnp.exp(4.0 / 3.0 * jnp.log(depth_now))
    friction_rate = GRAVITY * manning * manning * speed_now / powered
    return (speed_now, powered, friction_rate)

def salt_step(salt_adj, conductivity):
    zero_layer = jnp.zeros_like(salt_adj[:1])
    below_adj = jnp.concatenate([salt_adj[1:], zero_layer], 0)
    flux_down = conductivity * (below_adj - salt_adj)
    flux_up = jnp.concatenate([zero_layer, flux_down[:-1]], 0)
    return salt_adj + TIME_STEP * (flux_down - flux_up)

def window_sweep(adj_end, depth_win, velocity_win, salt_win, wet_win, cell_class, manning, conductivity):
    wet_f = wet_win.astype(jnp.float32)
    infiltration = wet_f * (0.25 + 0.75 * cell_class.astype(jnp.float32))
    surface_adj = adj_end[0]
    flow_x = adj_end[1]
    flow_y = adj_end[2]
    salt_adj = adj_end[3:]
    grad_n = jnp.zeros_like(surface_adj)
    grad_k = jnp.zeros_like(salt_adj)
    first_rate = None
    for step_now in range(depth_win.shape[0] - 1, -1, -1):
        depth_now = depth_win[step_now]
        velocity_now = velocity_win[step_now]
        speed_now, powered, friction_rate = friction(depth_now, velocity_now, manning)
        if step_now == 0:
            first_rate = friction_rate
        relaxed = 1.0 + TIME_STEP * friction_rate
        damping = wet_f / relaxed
        grad_n = grad_n - 2.0 * TIME_STEP * GRAVITY * manning * speed_now * (velocity_now[0] * flow_x + velocity_now[1] * flow_y) * damping / (powered * relaxed)
        salt_now = salt_win[step_now].astype(jnp.float32)
        zero_layer = jnp.zeros_like(salt_now[:1])
        salt_below = jnp.concatenate([salt_now[1:], zero_layer], 0)
        adj_below = jnp.concatenate([salt_adj[1:], zero_layer], 0)
        grad_k = grad_k + TIME_STEP * (salt_below - salt_now) * (salt_adj - adj_below)
        level_mid = surface_adj + TIME_STEP * lower_diff(depth_now * damping * flow_x, 0) + TIME_STEP * lower_diff(depth_now * damping * flow_y, 1)
        wet_mid = wet_f * level_mid
        flow_x = damping * flow_x + TIME_STEP * upper_diff(wet_mid, 0)
        flow_y = damping * flow_y + TIME_STEP * upper_diff(wet_mid, 1)
        surface_adj = level_mid + TIME_STEP * infiltration * salt_adj[0]
        salt_adj = salt_step(salt_adj, conductivity)
    steps_total = depth_win.shape[0]
    flow_factor = wet_f / (1.0 + steps_total * TIME_STEP * first_rate)
    cond_above = jnp.concatenate([jnp.zeros_like(conductivity[:1]), conductivity[:-1]], 0)
    salt_factor = 1.0 / (1.0 + steps_total * TIME_STEP * (conductivity + cond_above))
    coarse = jnp.concatenate([jnp.ones_like(surface_adj)[None], flow_factor[None], flow_factor[None], salt_factor], 0)
    fine_start = jnp.concatenate([surface_adj[None], flow_x[None], flow_y[None], salt_adj], 0)
    return (fine_start, coarse, grad_n, grad_k)

def reference(adjoint_end, depth_fwd, velocity_fwd, salt_fwd, wet_mask, cell_class, manning, conductivity):

    def per_window(window_items):
        return window_sweep(window_items[0], window_items[1], window_items[2], window_items[3], window_items[4], cell_class, manning, conductivity)
    fine_start, coarse, grad_n, grad_k = lax.map(per_window, (adjoint_end, depth_fwd, velocity_fwd, salt_fwd, wet_mask))
    offsets = fine_start - coarse * adjoint_end

    def link_step(end_new, link_items):
        start_new = link_items[0] * end_new + link_items[1]
        return (start_new, start_new)
    last_window = adjoint_end.shape[0] - 1
    unused, adjoint_start = lax.scan(link_step, adjoint_end[last_window], (coarse, offsets), reverse=True)
    return (adjoint_start, lax.optimization_barrier(jnp.sum(grad_n, axis=0)), lax.optimization_barrier(jnp.sum(grad_k, axis=0)))
```

```python
import jax
import jax.numpy as jnp
from jax import lax
from jax.experimental import pallas as pl
from jax.experimental.pallas import tpu as pltpu
from jax.sharding import PartitionSpec as P

TIME_STEP = 0.4
GRAVITY = 9.81
MESH = pl.DeviceIdType.MESH
F32 = jnp.float32


def remote(src, dst, send_sem, recv_sem, device):
    return pltpu.make_async_remote_copy(
        src_ref=src, dst_ref=dst, send_sem=send_sem, recv_sem=recv_sem,
        device_id=device, device_id_type=MESH,
    )


def kernel(
    space_n, end_ref, depth_ref, vel_ref, salt_ref, wet_ref, cls_ref, man_ref, cond_ref,
    out_ref, gn_ref, gk_ref,
    damp, hdamp, gcoef, source, off_s, fac_s, off_f, grads,
    down_out, up_out, down_in, up_in,
    core_s, core_f, pair_s, pair_f, z_s, z_f, quad_s, quad_f, y_s, y_f,
    zb_s_out, zb_f_out, zb_s, zb_f, eh_s, eh_f, cb_s_out, cb_f_out, cb_s, cb_f,
    core_g, sum_g, y_g, z_g_out, z_g,
    halo_sems, core_sems, z_sems, y_sems, yg_sems, zb_sems, cb_sems,
):
    sp = lax.axis_index("space")
    w = lax.axis_index("tm")
    core = lax.rem(w, 2)
    zh = lax.rem(lax.div(w, 2), 2)
    y = lax.div(w, 4)
    core_peer = (sp, w + 1 - 2 * core)
    z_peer = (sp, w + 2 - 4 * zh)
    has_prev = sp > 0
    has_next = sp < space_n - 1

    def y_peer(d):
        return (sp, lax.rem(w + 4 * d, 16))

    barrier = pltpu.get_barrier_semaphore()
    for peer in (core_peer, z_peer, y_peer(1), y_peer(2), y_peer(3)):
        pl.semaphore_signal(barrier, inc=1, device_id=peer, device_id_type=MESH)

    @pl.when(has_prev)
    def _():
        pl.semaphore_signal(barrier, inc=1, device_id=(sp - 1, w), device_id_type=MESH)

    @pl.when(has_next)
    def _():
        pl.semaphore_signal(barrier, inc=1, device_id=(sp + 1, w), device_id_type=MESH)

    last = jnp.where(w == 15, 1.0, 0.0).astype(F32)

    def chunk(i, carry):
        block = lax.div(i, 4)
        g_core = lax.rem(i, 2)
        g_zh = lax.rem(lax.div(i, 2), 2)
        cols = pl.ds(pl.multiple_of(i * 128, 128), 128)
        sub = pl.ds(pl.multiple_of(lax.rem(i, 4) * 128, 128), 128)
        wet = wet_ref[0, :, cols].astype(F32)
        infil = TIME_STEP * wet * (0.25 + 0.75 * cls_ref[:, cols].astype(F32))
        man = man_ref[:, cols]
        cond = cond_ref[:, :, cols]
        mu = end_ref[0, 3:, :, cols]
        zero = jnp.zeros_like(mu[:1])
        cond_above = jnp.concatenate([zero, cond[:-1]], 0)
        factor = 1.0 / (1.0 + 4 * TIME_STEP * (cond + cond_above))
        gk = jnp.zeros_like(mu)
        start = mu
        for k in (3, 2, 1, 0):
            h = depth_ref[0, k, :, cols]
            u = vel_ref[0, k, 0, :, cols]
            v = vel_ref[0, k, 1, :, cols]
            speed = jnp.sqrt(u * u + v * v)
            powered = jnp.exp(4.0 / 3.0 * jnp.log(h))
            rate = GRAVITY * man * man * speed / powered
            relaxed = 1.0 + TIME_STEP * rate
            damping = wet / relaxed
            damp[k, :, cols] = damping
            hdamp[k, :, cols] = h * damping
            gcoef[k, :, cols] = (
                -2.0 * TIME_STEP * GRAVITY * man * speed * damping / (powered * relaxed)
            )
            if k == 0:
                off_f[block, 3, :, sub] = wet / (1.0 + 4 * TIME_STEP * rate)
            source[k, :, cols] = infil * mu[0]
            salt = salt_ref[0, k, :, :, cols].astype(F32)
            salt_below = jnp.concatenate([salt[1:], zero], 0)
            mu_below = jnp.concatenate([mu[1:], zero], 0)
            diff = mu_below - mu
            gk = gk - TIME_STEP * (salt_below - salt) * diff
            flux = cond * diff
            mu = mu + TIME_STEP * (flux - jnp.concatenate([zero, flux[:-1]], 0))
        held = factor * start
        offset = mu - held
        off_s[block, :, :, sub] = offset + last * held
        fac_s[block, :, :, sub] = factor
        grads[g_core, block, g_zh, 0:8] = gk
        return carry

    lax.fori_loop(0, 16, chunk, 0)

    for d in (1, 2, 3):
        @pl.when(y + d > 3)
        def _(d=d):
            y_s[d - 1] = jnp.zeros(y_s.shape[1:], F32)
            y_f[d - 1] = jnp.zeros(y_f.shape[1:], F32)

    @pl.when(sp == 0)
    def _():
        down_in[...] = jnp.zeros(down_in.shape, F32)

    @pl.when(sp == space_n - 1)
    def _():
        up_in[...] = jnp.zeros(up_in.shape, F32)

    pl.semaphore_wait(
        barrier, 5 + jnp.where(has_prev, 1, 0) + jnp.where(has_next, 1, 0)
    )

    other_half = pl.ds(2 * (1 - core), 2)
    copy_core_s = remote(
        off_s.at[other_half], core_s, core_sems.at[0, 0], core_sems.at[1, 0], core_peer
    )
    copy_core_s.start()
    copy_z_s = remote(pair_s.at[1 - zh], z_s, z_sems.at[0, 0], z_sems.at[1, 0], z_peer)
    copy_z_f = remote(pair_f.at[1 - zh], z_f, z_sems.at[0, 1], z_sems.at[1, 1], z_peer)

    def pair_salt():
        copy_core_s.wait_recv()
        for b in range(2):
            mine = off_s[2 * core + b]
            theirs = core_s[b]
            earlier = jnp.where(core == 0, mine, theirs)
            later = jnp.where(core == 0, theirs, mine)
            pair_s[b] = earlier + fac_s[2 * core + b] * later
        copy_z_s.start()

    level = end_ref[0, 0]
    flow_x = end_ref[0, 1]
    flow_y = end_ref[0, 2]
    wet = wet_ref[0].astype(F32)
    lanes = lax.broadcasted_iota(jnp.int32, level.shape, 1)
    n_cols = level.shape[1]
    grad_n = jnp.zeros_like(level)
    halo_copies = []
    for turn, k in enumerate((3, 2, 1, 0)):
        hdx = hdamp[k] * flow_x
        hdy = hdamp[k] * flow_y
        hdy_left = jnp.where(lanes == 0, 0.0, pltpu.roll(hdy, 1, 1))
        partial = level + TIME_STEP * hdx + TIME_STEP * (hdy - hdy_left)
        down_out[turn] = hdx[3:4]
        up_out[turn, 0:1] = wet[0:1] * partial[0:1]
        up_out[turn, 1:2] = wet[0:1]
        down = remote(
            down_out.at[turn], down_in.at[turn],
            halo_sems.at[0, turn], halo_sems.at[1, turn], (sp + 1, w),
        )
        up = remote(
            up_out.at[turn], up_in.at[turn],
            halo_sems.at[2, turn], halo_sems.at[3, turn], (sp - 1, w),
        )
        halo_copies.append((down, up))

        @pl.when(has_next)
        def _(down=down):
            down.start()

        @pl.when(has_prev)
        def _(up=up):
            up.start()

        if turn == 0:
            pair_salt()
        grad_n = grad_n + gcoef[k] * (vel_ref[0, k, 0] * flow_x + vel_ref[0, k, 1] * flow_y)

        @pl.when(has_prev)
        def _(down=down):
            down.wait_recv()

        @pl.when(has_next)
        def _(up=up):
            up.wait_recv()

        before = jnp.concatenate([down_in[turn], hdx[0:3]], 0)
        mid = partial - TIME_STEP * before
        wet_mid = wet * mid
        after_row = up_in[turn, 0:1] - TIME_STEP * up_in[turn, 1:2] * hdx[3:4]
        after = jnp.concatenate([wet_mid[1:4], after_row], 0)
        right = jnp.where(lanes == n_cols - 1, 0.0, pltpu.roll(wet_mid, n_cols - 1, 1))
        damping = damp[k]
        flow_x = damping * flow_x + TIME_STEP * (after - wet_mid)
        flow_y = damping * flow_y + TIME_STEP * (right - wet_mid)
        level = mid + source[k]

    for b in range(4):
        cols = slice(b * 512, b * 512 + 512)
        factor = off_f[b, 3]
        off_f[b, 0] = level[:, cols] - (1.0 - last) * end_ref[0, 0, :, cols]
        off_f[b, 1] = flow_x[:, cols] - (1.0 - last) * factor * end_ref[0, 1, :, cols]
        off_f[b, 2] = flow_y[:, cols] - (1.0 - last) * factor * end_ref[0, 2, :, cols]
    copy_core_f = remote(
        off_f.at[other_half], core_f, core_sems.at[0, 1], core_sems.at[1, 1], core_peer
    )
    copy_core_f.start()
    for i in range(16):
        grads[i % 2, i // 4, i // 2 % 2, 8] = grad_n[:, i * 128 : i * 128 + 128]
    copy_core_g = remote(
        grads.at[1 - core], core_g, core_sems.at[0, 2], core_sems.at[1, 2], core_peer
    )
    copy_core_g.start()

    copy_core_f.wait_recv()
    for b in range(2):
        mine = off_f[2 * core + b]
        theirs = core_f[b]
        earlier = jnp.where(core == 0, mine, theirs)
        later = jnp.where(core == 0, theirs, mine)
        pair_f[b, 0] = earlier[0] + later[0]
        pair_f[b, 1] = earlier[1] + earlier[3] * later[1]
        pair_f[b, 2] = earlier[2] + earlier[3] * later[2]
        pair_f[b, 3] = earlier[3] * later[3]
    copy_z_f.start()

    def y_copies(quad, slots, which):
        return [
            remote(
                quad, slots.at[d - 1], y_sems.at[0, which, d - 1], y_sems.at[1, which, d - 1],
                y_peer(4 - d),
            )
            for d in (1, 2, 3)
        ]

    def start_down(copies):
        for d in (1, 2, 3):
            @pl.when(y >= d)
            def _(d=d):
                copies[d - 1].start()

    def wait_down(copies):
        for d in (1, 2, 3):
            @pl.when(y + d <= 3)
            def _(d=d):
                copies[d - 1].wait_recv()

    own = 2 * core + zh
    copy_z_s.wait_recv()
    factor = fac_s[own]
    pair_factor = factor * factor
    mine = pair_s[zh]
    theirs = z_s[...]
    pair_first = jnp.where(zh == 0, mine, theirs)
    pair_second = jnp.where(zh == 0, theirs, mine)
    quad_s[...] = pair_first + pair_factor * pair_second
    copies_y_s = y_copies(quad_s, y_s, 0)
    start_down(copies_y_s)

    copy_core_g.wait_recv()
    sum_g[...] = grads[core] + core_g[...]
    copies_y_g = []
    for d in (1, 2, 3):
        copy = remote(
            sum_g.at[lax.rem(y + d, 4)], y_g.at[d - 1],
            yg_sems.at[0, d - 1], yg_sems.at[1, d - 1], y_peer(d),
        )
        copy.start()
        copies_y_g.append(copy)

    copy_zb_s = remote(zb_s_out, zb_s, zb_sems.at[0, 0], zb_sems.at[1, 0], z_peer)
    copy_zb_f = remote(zb_f_out, zb_f, zb_sems.at[0, 1], zb_sems.at[1, 1], z_peer)
    copy_zb_g = remote(z_g_out.at[1 - zh], z_g, zb_sems.at[0, 2], zb_sems.at[1, 2], z_peer)

    wait_down(copies_y_s)
    factor = fac_s[own]
    pair_factor = factor * factor
    quad_factor = pair_factor * pair_factor
    at_second = y_s[0] + quad_factor * (y_s[1] + quad_factor * y_s[2])
    mine = pair_s[zh]
    theirs = z_s[...]
    at_first = jnp.where(zh == 0, theirs, mine) + pair_factor * at_second
    eh_s[zh] = jnp.where(zh == 0, at_first, at_second)
    zb_s_out[...] = jnp.where(zh == 0, at_second, at_first)
    copy_zb_s.start()

    copy_z_f.wait_recv()
    mine = pair_f[zh]
    theirs = z_f[...]
    first_f = jnp.where(zh == 0, mine, theirs)
    second_f = jnp.where(zh == 0, theirs, mine)
    quad_f[0] = first_f[0] + second_f[0]
    quad_f[1] = first_f[1] + first_f[3] * second_f[1]
    quad_f[2] = first_f[2] + first_f[3] * second_f[2]
    quad_f[3] = first_f[3] * second_f[3]
    copies_y_f = y_copies(quad_f, y_f, 1)
    start_down(copies_y_f)

    total = sum_g[y]
    for d in (1, 2, 3):
        copies_y_g[d - 1].wait_recv()
        total = total + y_g[d - 1]
    z_g_out[...] = total
    copy_zb_g.start()

    wait_down(copies_y_f)
    mine = pair_f[zh]
    theirs = z_f[...]
    second_f = jnp.where(zh == 0, theirs, mine)
    for field in range(3):
        if field == 0:
            at_second = y_f[0, 0] + y_f[1, 0] + y_f[2, 0]
            at_first = second_f[0] + at_second
        else:
            at_second = y_f[0, field] + y_f[0, 3] * (
                y_f[1, field] + y_f[1, 3] * y_f[2, field]
            )
            at_first = second_f[field] + second_f[3] * at_second
        eh_f[zh, field] = jnp.where(zh == 0, at_first, at_second)
        zb_f_out[field] = jnp.where(zh == 0, at_second, at_first)
    copy_zb_f.start()

    copy_zb_s.wait_recv()
    eh_s[1 - zh] = zb_s[...]
    for b in range(2):
        late = eh_s[b]
        mine = off_s[2 * core + b]
        theirs = core_s[b]
        early = jnp.where(core == 0, theirs, mine) + fac_s[2 * core + b] * late
        cb_s_out[b] = jnp.where(core == 0, late, early)
        eh_s[b] = jnp.where(core == 0, early, late)
    copy_cb_s = remote(cb_s_out, cb_s, cb_sems.at[0, 0], cb_sems.at[1, 0], core_peer)
    copy_cb_s.start()
    for b in range(2):
        block = 2 * core + b
        cols = pl.ds(pl.multiple_of(block * 512, 512), 512)
        out_ref[0, 3:, :, cols] = off_s[block] + fac_s[block] * eh_s[b]

    copy_zb_f.wait_recv()
    eh_f[1 - zh] = zb_f[...]
    for b in range(2):
        mine = off_f[2 * core + b]
        theirs = core_f[b]
        late_map = jnp.where(core == 0, theirs, mine)
        for field in range(3):
            late = eh_f[b, field]
            if field == 0:
                early = late_map[0] + late
            else:
                early = late_map[field] + late_map[3] * late
            cb_f_out[b, field] = jnp.where(core == 0, late, early)
            eh_f[b, field] = jnp.where(core == 0, early, late)
    copy_cb_f = remote(cb_f_out, cb_f, cb_sems.at[0, 1], cb_sems.at[1, 1], core_peer)
    copy_cb_f.start()

    copy_zb_g.wait_recv()
    total = z_g_out[zh] + z_g[...]
    gk_ref[...] = total[0:8]
    gn_ref[...] = total[8]

    copy_cb_s.wait_recv()
    for b in range(2):
        block = 2 * (1 - core) + b
        cols = pl.ds(pl.multiple_of(block * 512, 512), 512)
        out_ref[0, 3:, :, cols] = off_s[block] + fac_s[block] * cb_s[b]
    copy_cb_f.wait_recv()
    for half in range(2):
        for b in range(2):
            block = 2 * core + b if half == 0 else 2 * (1 - core) + b
            cols = pl.ds(pl.multiple_of(block * 512, 512), 512)
            ends = eh_f if half == 0 else cb_f
            factor = off_f[block, 3]
            out_ref[0, 0, :, cols] = off_f[block, 0] + ends[b, 0]
            out_ref[0, 1, :, cols] = off_f[block, 1] + factor * ends[b, 1]
            out_ref[0, 2, :, cols] = off_f[block, 2] + factor * ends[b, 2]

    for down, up in halo_copies:
        @pl.when(has_next)
        def _(down=down):
            down.wait_send()

        @pl.when(has_prev)
        def _(up=up):
            up.wait_send()

    for d in (1, 2, 3):
        @pl.when(y >= d)
        def _(d=d):
            copies_y_s[d - 1].wait_send()
            copies_y_f[d - 1].wait_send()

    for copy in copies_y_g + [
        copy_core_s, copy_core_f, copy_core_g, copy_z_s, copy_z_f,
        copy_zb_s, copy_zb_f, copy_zb_g, copy_cb_s, copy_cb_f,
    ]:
        copy.wait_send()


def body(space_n, *args):
    def kern(*refs):
        kernel(space_n, *refs)

    def vmem(*shape):
        return pltpu.VMEM(shape, F32)

    def sems(*shape):
        return pltpu.SemaphoreType.DMA(shape)

    start, grad_n, grad_k = pl.pallas_call(
        kern,
        out_shape=(
            jax.ShapeDtypeStruct((1, 11, 4, 2048), F32),
            jax.ShapeDtypeStruct((4, 128), F32),
            jax.ShapeDtypeStruct((8, 4, 128), F32),
        ),
        in_specs=[pl.BlockSpec(memory_space=pltpu.VMEM)] * 8,
        out_specs=[pl.BlockSpec(memory_space=pltpu.VMEM)] * 3,
        scratch_shapes=[
            vmem(4, 4, 2048), vmem(4, 4, 2048), vmem(4, 4, 2048), vmem(4, 4, 2048),
            vmem(4, 8, 4, 512), vmem(4, 8, 4, 512), vmem(4, 4, 4, 512),
            vmem(2, 4, 2, 9, 4, 128),
            vmem(4, 1, 2048), vmem(4, 2, 2048), vmem(4, 1, 2048), vmem(4, 2, 2048),
            vmem(2, 8, 4, 512), vmem(2, 4, 4, 512), vmem(2, 8, 4, 512), vmem(2, 4, 4, 512),
            vmem(8, 4, 512), vmem(4, 4, 512), vmem(8, 4, 512), vmem(4, 4, 512),
            vmem(3, 8, 4, 512), vmem(3, 4, 4, 512),
            vmem(8, 4, 512), vmem(3, 4, 512), vmem(8, 4, 512), vmem(3, 4, 512),
            vmem(2, 8, 4, 512), vmem(2, 3, 4, 512),
            vmem(2, 8, 4, 512), vmem(2, 3, 4, 512), vmem(2, 8, 4, 512), vmem(2, 3, 4, 512),
            vmem(4, 2, 9, 4, 128), vmem(4, 2, 9, 4, 128), vmem(3, 2, 9, 4, 128),
            vmem(2, 9, 4, 128), vmem(9, 4, 128),
            sems(4, 4), sems(2, 3), sems(2, 2), sems(2, 2, 3), sems(2, 3), sems(2, 3),
            sems(2, 2),
        ],
        compiler_params=pltpu.CompilerParams(collective_id=0, has_side_effects=True),
    )(*args)
    return start, grad_n, grad_k


def solution(mesh):
    space_n = mesh.shape["space"]

    def local(*args):
        return body(space_n, *args)

    return jax.shard_map(
        local,
        mesh=mesh,
        in_specs=(
            P("tm", None, "space", None),
            P("tm", None, "space", None),
            P("tm", None, None, "space", None),
            P("tm", None, None, "space", None),
            P("tm", "space", None),
            P("space", None),
            P("space", None),
            P(None, "space", None),
        ),
        out_specs=(P("tm", None, "space", None), P("space", "tm"), P(None, "space", "tm")),
        check_vma=False,
    )
```

```python
import jax
import jax.numpy as jnp
from jax import lax
from jax.experimental import pallas as pl
from jax.experimental.pallas import tpu as pltpu
from jax.sharding import PartitionSpec as P

TIME_STEP = 0.4
GRAVITY = 9.81
MESH = pl.DeviceIdType.MESH
F32 = jnp.float32


def remote(src, dst, send_sem, recv_sem, device):
    return pltpu.make_async_remote_copy(
        src_ref=src, dst_ref=dst, send_sem=send_sem, recv_sem=recv_sem,
        device_id=device, device_id_type=MESH,
    )


def kernel(
    space_n, end_hbm, depth_hbm, vel_hbm, salt_hbm, wet_hbm, cls_hbm, man_hbm, cond_hbm,
    out_ref, gn_ref, gk_ref,
    end_ref, depth_ref, vel_ref, salt_ref, wet_ref, cls_ref, man_ref, cond_ref,
    damp, hdamp, gcoef, source, fac_s, grads,
    down_out, up_out, down_in, up_in,
    off_0, core_0, pair_0, z_0, quad_0, y_0, back_0, home_0,
    off_1, core_1, pair_1, z_1, quad_1, y_1, back_1, home_1,
    off_f, core_f, pair_f, z_f, quad_f, y_f, back_f, home_f,
    core_g, sum_g, y_g, z_g_out, z_g,
    in_sems, halo_sems, core_sems, z_sems, y_sems, back_sems,
):
    sp = lax.axis_index("space")
    w = lax.axis_index("tm")
    core = lax.rem(w, 2)
    zh = lax.rem(lax.div(w, 2), 2)
    y = lax.div(w, 4)
    core_peer = (sp, w + 1 - 2 * core)
    z_peer = (sp, w + 2 - 4 * zh)
    has_prev = sp > 0
    has_next = sp < space_n - 1

    def y_peer(d):
        return (sp, lax.rem(w + 4 * d, 16))

    barrier = pltpu.get_barrier_semaphore()
    for peer in (z_peer, core_peer, y_peer(1), y_peer(2), y_peer(3)):
        pl.semaphore_signal(barrier, inc=1, device_id=peer, device_id_type=MESH)

    @pl.when(has_prev)
    def _():
        pl.semaphore_signal(barrier, inc=1, device_id=(sp - 1, w), device_id_type=MESH)

    @pl.when(has_next)
    def _():
        pl.semaphore_signal(barrier, inc=1, device_id=(sp + 1, w), device_id_type=MESH)

    loads = []
    for at, (src, dst) in enumerate((
        (end_hbm, end_ref), (depth_hbm, depth_ref), (vel_hbm, vel_ref), (salt_hbm, salt_ref),
        (wet_hbm, wet_ref), (cls_hbm, cls_ref), (man_hbm, man_ref), (cond_hbm, cond_ref),
    )):
        load = pltpu.make_async_copy(src, dst, in_sems.at[at])
        load.start()
        loads.append(load)

    last = jnp.where(w == 15, 1.0, 0.0).astype(F32)

    for d in (1, 2, 3):
        @pl.when(y + d > 3)
        def _(d=d):
            for slots in (y_0, y_1, y_f):
                slots[d - 1] = jnp.zeros(slots.shape[1:], F32)

    @pl.when(sp == 0)
    def _():
        down_in[...] = jnp.zeros(down_in.shape, F32)

    @pl.when(sp == space_n - 1)
    def _():
        up_in[...] = jnp.zeros(up_in.shape, F32)

    for load in loads:
        load.wait()

    def chunk(i, carry):
        block = lax.div(i, 4)
        g_core = lax.rem(i, 2)
        g_zh = lax.rem(lax.div(i, 2), 2)
        cols = pl.ds(pl.multiple_of(i * 128, 128), 128)
        sub = pl.ds(pl.multiple_of(lax.rem(i, 4) * 128, 128), 128)
        wet = wet_ref[0, :, cols].astype(F32)
        infil = TIME_STEP * wet * (0.25 + 0.75 * cls_ref[:, cols].astype(F32))
        man = man_ref[:, cols]
        cond = cond_ref[:, :, cols]
        mu = end_ref[0, 3:, :, cols]
        zero = jnp.zeros_like(mu[:1])
        cond_above = jnp.concatenate([zero, cond[:-1]], 0)
        factor = 1.0 / (1.0 + 4 * TIME_STEP * (cond + cond_above))
        gk = jnp.zeros_like(mu)
        start = mu
        for k in (3, 2, 1, 0):
            h = depth_ref[0, k, :, cols]
            u = vel_ref[0, k, 0, :, cols]
            v = vel_ref[0, k, 1, :, cols]
            speed = jnp.sqrt(u * u + v * v)
            powered = jnp.exp(4.0 / 3.0 * jnp.log(h))
            rate = GRAVITY * man * man * speed / powered
            relaxed = 1.0 + TIME_STEP * rate
            damping = wet / relaxed
            damp[k, :, cols] = damping
            hdamp[k, :, cols] = h * damping
            gcoef[k, :, cols] = (
                -2.0 * TIME_STEP * GRAVITY * man * speed * damping / (powered * relaxed)
            )
            if k == 0:
                off_0[block, 4, :, sub] = wet / (1.0 + 4 * TIME_STEP * rate)
            source[k, :, cols] = infil * mu[0]
            salt = salt_ref[0, k, :, :, cols].astype(F32)
            salt_below = jnp.concatenate([salt[1:], zero], 0)
            mu_below = jnp.concatenate([mu[1:], zero], 0)
            diff = mu_below - mu
            gk = gk - TIME_STEP * (salt_below - salt) * diff
            flux = cond * diff
            mu = mu + TIME_STEP * (flux - jnp.concatenate([zero, flux[:-1]], 0))
        held = factor * start
        offset = mu - held
        offset = offset + last * held
        off_0[block, 0:4, :, sub] = offset[0:4]
        off_1[block, :, :, sub] = offset[4:8]
        fac_s[block, :, :, sub] = factor
        grads[g_core, block, g_zh, 0:8] = gk
        return carry

    lax.fori_loop(0, 16, chunk, 0)

    pl.semaphore_wait(
        barrier, 5 + jnp.where(has_prev, 1, 0) + jnp.where(has_next, 1, 0)
    )

    other_half = pl.ds(2 * (1 - core), 2)
    waves = (
        (off_0, core_0, pair_0, z_0, quad_0, y_0, back_0, home_0),
        (off_1, core_1, pair_1, z_1, quad_1, y_1, back_1, home_1),
        (off_f, core_f, pair_f, z_f, quad_f, y_f, back_f, home_f),
    )
    core_copies = [
        remote(v[0].at[other_half], v[1], core_sems.at[0, i], core_sems.at[1, i], core_peer)
        for i, v in enumerate(waves)
    ]
    z_copies = [
        remote(v[2], v[3], z_sems.at[0, i], z_sems.at[1, i], z_peer)
        for i, v in enumerate(waves)
    ]
    y_copies = [
        [
            remote(v[4], v[5].at[d - 1], y_sems.at[0, i, d - 1], y_sems.at[1, i, d - 1],
                   y_peer(4 - d))
            for d in (1, 2, 3)
        ]
        for i, v in enumerate(waves)
    ]
    back_copies = [
        remote(v[6], v[7], back_sems.at[0, i], back_sems.at[1, i], core_peer)
        for i, v in enumerate(waves)
    ]

    def core_flow(b):
        mine = off_0[2 * core + b, 4]
        theirs = core_0[b, 4]
        return jnp.where(core == 0, mine, theirs), jnp.where(core == 0, theirs, mine)

    def z_flow(b):
        mine = pair_0[b, 4]
        theirs = z_0[b, 4]
        return jnp.where(zh == 0, mine, theirs), jnp.where(zh == 0, theirs, mine)

    def factors(i, b):
        return fac_s[2 * core + b, 4 * i : 4 * i + 4]

    def make_pair(i):
        off, arrived, pair = waves[i][:3]
        core_copies[i].wait_recv()
        for b in range(2):
            mine = off[2 * core + b]
            theirs = arrived[b]
            earlier = jnp.where(core == 0, mine, theirs)
            later = jnp.where(core == 0, theirs, mine)
            if i == 2:
                factor, _ = core_flow(b)
                pair[b, 0] = earlier[0] + later[0]
                pair[b, 1:3] = earlier[1:3] + factor[None] * later[1:3]
            else:
                pair[b, 0:4] = earlier[0:4] + factors(i, b) * later[0:4]
                if i == 0:
                    pair[b, 4] = earlier[4] * later[4]
        z_copies[i].start()

    def make_quad(i):
        pair, arrived, quad = waves[i][2:5]
        z_copies[i].wait_recv()
        for b in range(2):
            mine = pair[b]
            theirs = arrived[b]
            earlier = jnp.where(zh == 0, mine, theirs)
            later = jnp.where(zh == 0, theirs, mine)
            if i == 2:
                factor, _ = z_flow(b)
                quad[b, 0] = earlier[0] + later[0]
                quad[b, 1:3] = earlier[1:3] + factor[None] * later[1:3]
            else:
                factor = factors(i, b)
                quad[b, 0:4] = earlier[0:4] + factor * factor * later[0:4]
                if i == 0:
                    quad[b, 4] = earlier[4] * later[4]
        for d in (1, 2, 3):
            @pl.when(y >= d)
            def _(d=d):
                y_copies[i][d - 1].start()

    def results(i, block, offset, ends):
        cols = pl.ds(pl.multiple_of(block * 512, 512), 512)
        if i == 2:
            out_ref[0, 0, :, cols] = offset[0] + ends[0]
            out_ref[0, 1:3, :, cols] = offset[1:3] + off_0[block, 4][None] * ends[1:3]
        else:
            factor = fac_s[block, 4 * i : 4 * i + 4]
            out_ref[0, 3 + 4 * i : 7 + 4 * i, :, cols] = offset[0:4] + factor * ends

    def make_ends(i):
        off, arrived, pair, z_arrived, _, slots, back = waves[i][:7]
        for d in (1, 2, 3):
            @pl.when(y + d <= 3)
            def _(d=d):
                y_copies[i][d - 1].wait_recv()
        own_ends = []
        for b in range(2):
            mine = off[2 * core + b]
            first = jnp.where(core == 0, arrived[b], mine)
            second = jnp.where(zh == 0, z_arrived[b], pair[b])
            if i == 2:
                _, core_factor = core_flow(b)
                _, z_factor = z_flow(b)

                def through(factor, map_, end):
                    return jnp.concatenate(
                        [map_[0:1] + end[0:1], map_[1:3] + factor[None] * end[1:3]], 0
                    )

                at_second = through(y_0[1, b, 4], slots[1, b], slots[2, b])
                at_second = through(y_0[0, b, 4], slots[0, b], at_second)
                at_first = through(z_factor, second, at_second)
                late = jnp.where(zh == 0, at_first, at_second)
                early = through(core_factor, first, late)
            else:
                factor = factors(i, b)
                two = factor * factor
                four = two * two
                at_second = slots[0, b, 0:4] + four * (
                    slots[1, b, 0:4] + four * slots[2, b, 0:4]
                )
                at_first = second[0:4] + two * at_second
                late = jnp.where(zh == 0, at_first, at_second)
                early = first[0:4] + factor * late
            back[b] = jnp.where(core == 0, late, early)
            own_ends.append((mine, jnp.where(core == 0, early, late)))
        back_copies[i].start()
        for b, (mine, ends) in enumerate(own_ends):
            results(i, 2 * core + b, mine, ends)

    def finish(i):
        back_copies[i].wait_recv()
        for b in range(2):
            block = 2 * (1 - core) + b
            results(i, block, waves[i][0][block], waves[i][7][b])

    core_copies[0].start()
    core_copies[1].start()

    level = end_ref[0, 0]
    flow_x = end_ref[0, 1]
    flow_y = end_ref[0, 2]
    wet = wet_ref[0].astype(F32)
    n_cols = level.shape[1]
    grad_n = jnp.zeros_like(level)
    halo_copies = []

    def left(value):
        lanes = lax.broadcasted_iota(jnp.int32, value.shape, 1)
        return jnp.where(lanes == 0, 0.0, pltpu.roll(value, 1, 1))

    def right(value):
        lanes = lax.broadcasted_iota(jnp.int32, value.shape, 1)
        return jnp.where(lanes == n_cols - 1, 0.0, pltpu.roll(value, n_cols - 1, 1))

    def without_above(k, level, flow_x, flow_y):
        hdx = hdamp[k] * flow_x
        hdy = hdamp[k] * flow_y
        return hdx, level + TIME_STEP * hdx + TIME_STEP * (hdy - left(hdy))

    def advance(k, partial, hdx, above, below, flow_x, flow_y):
        mid = partial - TIME_STEP * jnp.concatenate([above, hdx[0:3]], 0)
        wet_mid = wet * mid
        after = jnp.concatenate([wet_mid[1:4], below], 0)
        damping = damp[k]
        return (
            mid + source[k],
            damping * flow_x + TIME_STEP * (after - wet_mid),
            damping * flow_y + TIME_STEP * (right(wet_mid) - wet_mid),
            wet_mid,
        )

    def friction_term(k, flow_x, flow_y):
        return gcoef[k] * (vel_ref[0, k, 0] * flow_x + vel_ref[0, k, 1] * flow_y)

    for turn, (k, k_next) in enumerate(((3, 2), (1, 0))):
        hdx, partial = without_above(k, level, flow_x, flow_y)
        first, second, third, fourth = (slice(r, r + 1) for r in range(4))
        wet_mid_3 = wet[fourth] * (partial[fourth] - TIME_STEP * hdx[third])
        held_x = damp[k] * flow_x
        hd_next = hdamp[k_next]
        down_out[turn, 0:1] = hdx[fourth]
        down_out[turn, 1:2] = hd_next[fourth] * (held_x[fourth] - TIME_STEP * wet_mid_3)
        down_out[turn, 2:3] = TIME_STEP * hd_next[fourth]
        wet_mid_0 = wet[first] * partial[first]
        wet_mid_1 = wet[second] * (partial[second] - TIME_STEP * hdx[first])
        row_x = held_x[first] + TIME_STEP * (wet_mid_1 - wet_mid_0)
        row_y = damp[k, 0:1] * flow_y[first] + TIME_STEP * (right(wet_mid_0) - wet_mid_0)
        row_hdy = hd_next[first] * row_y
        up_out[turn, 0:1] = wet_mid_0
        up_out[turn, 1:2] = wet[first]
        up_out[turn, 2:3] = (
            partial[first] + source[k, 0:1] + TIME_STEP * hd_next[first] * row_x
            + TIME_STEP * (row_hdy - left(row_hdy))
        )
        up_out[turn, 3:4] = hd_next[first]
        down = remote(
            down_out.at[turn], down_in.at[turn],
            halo_sems.at[0, turn], halo_sems.at[1, turn], (sp + 1, w),
        )
        up = remote(
            up_out.at[turn], up_in.at[turn],
            halo_sems.at[2, turn], halo_sems.at[3, turn], (sp - 1, w),
        )
        halo_copies.append((down, up))

        @pl.when(has_next)
        def _(down=down):
            down.start()

        @pl.when(has_prev)
        def _(up=up):
            up.start()

        if turn == 0:
            make_pair(0)
            make_pair(1)
        grad_n = grad_n + friction_term(k, flow_x, flow_y)

        @pl.when(has_prev)
        def _(down=down):
            down.wait_recv()

        @pl.when(has_next)
        def _(up=up):
            up.wait_recv()

        wet_4 = up_in[turn, 1:2]
        hd_4 = up_in[turn, 3:4]
        added = -TIME_STEP * hdx[fourth]
        wet_added = wet_4 * added
        added_y = hd_4 * (TIME_STEP * (right(wet_added) - wet_added))
        partial_4 = (
            up_in[turn, 2:3] + added - TIME_STEP * TIME_STEP * hd_4 * wet_added
            + TIME_STEP * (added_y - left(added_y))
        )
        level, flow_x, flow_y, wet_mid = advance(
            k, partial, hdx, down_in[turn, 0:1], up_in[turn, 0:1] + wet_added, flow_x, flow_y
        )
        grad_n = grad_n + friction_term(k_next, flow_x, flow_y)
        hdx, partial = without_above(k_next, level, flow_x, flow_y)
        above = down_in[turn, 1:2] + down_in[turn, 2:3] * wet_mid[first]
        below = wet_4 * (partial_4 - TIME_STEP * hdx[fourth])
        level, flow_x, flow_y, _ = advance(
            k_next, partial, hdx, above, below, flow_x, flow_y
        )

    for b in range(4):
        cols = slice(b * 512, b * 512 + 512)
        factor = off_0[b, 4]
        off_f[b, 0] = level[:, cols] - (1.0 - last) * end_ref[0, 0, :, cols]
        off_f[b, 1] = flow_x[:, cols] - (1.0 - last) * factor * end_ref[0, 1, :, cols]
        off_f[b, 2] = flow_y[:, cols] - (1.0 - last) * factor * end_ref[0, 2, :, cols]
    core_copies[2].start()
    for i in range(16):
        grads[i % 2, i // 4, i // 2 % 2, 8] = grad_n[:, i * 128 : i * 128 + 128]
    copy_core_g = remote(
        grads.at[1 - core], core_g, core_sems.at[0, 3], core_sems.at[1, 3], core_peer
    )
    copy_core_g.start()

    make_pair(2)
    copy_core_g.wait_recv()
    sum_g[...] = grads[core] + core_g[...]
    copies_y_g = []
    for d in (1, 2, 3):
        copy = remote(
            sum_g.at[lax.rem(y + d, 4)], y_g.at[d - 1],
            y_sems.at[0, 3, d - 1], y_sems.at[1, 3, d - 1], y_peer(d),
        )
        copy.start()
        copies_y_g.append(copy)
    copy_z_g = remote(z_g_out.at[1 - zh], z_g, z_sems.at[0, 3], z_sems.at[1, 3], z_peer)

    make_quad(0)
    make_quad(1)
    total = sum_g[y]
    for d in (1, 2, 3):
        copies_y_g[d - 1].wait_recv()
        total = total + y_g[d - 1]
    z_g_out[...] = total
    copy_z_g.start()
    make_ends(0)
    make_quad(2)
    make_ends(1)
    copy_z_g.wait_recv()
    total = z_g_out[zh] + z_g[...]
    gk_ref[...] = total[0:8]
    gn_ref[...] = total[8]
    finish(0)
    make_ends(2)
    finish(1)
    finish(2)

    for down, up in halo_copies:
        @pl.when(has_next)
        def _(down=down):
            down.wait_send()

        @pl.when(has_prev)
        def _(up=up):
            up.wait_send()

    for d in (1, 2, 3):
        @pl.when(y >= d)
        def _(d=d):
            for copies in y_copies:
                copies[d - 1].wait_send()

    for copy in core_copies + z_copies + back_copies + copies_y_g + [copy_core_g, copy_z_g]:
        copy.wait_send()


def body(space_n, *args):
    def kern(*refs):
        kernel(space_n, *refs)

    def vmem(*shape):
        return pltpu.VMEM(shape, F32)

    def sems(*shape):
        return pltpu.SemaphoreType.DMA(shape)

    def wave(maps, ends):
        return [
            vmem(4, maps, 4, 512), vmem(2, maps, 4, 512), vmem(2, maps, 4, 512),
            vmem(2, maps, 4, 512), vmem(2, maps, 4, 512), vmem(3, 2, maps, 4, 512),
            vmem(2, ends, 4, 512), vmem(2, ends, 4, 512),
        ]

    start, grad_n, grad_k = pl.pallas_call(
        kern,
        out_shape=(
            jax.ShapeDtypeStruct((1, 11, 4, 2048), F32),
            jax.ShapeDtypeStruct((4, 128), F32),
            jax.ShapeDtypeStruct((8, 4, 128), F32),
        ),
        in_specs=[pl.BlockSpec(memory_space=pl.ANY)] * 8,
        out_specs=[pl.BlockSpec(memory_space=pltpu.VMEM)] * 3,
        scratch_shapes=[
            *[pltpu.VMEM(a.shape, a.dtype) for a in args],
            vmem(4, 4, 2048), vmem(4, 4, 2048), vmem(4, 4, 2048), vmem(4, 4, 2048),
            vmem(4, 8, 4, 512), vmem(2, 4, 2, 9, 4, 128),
            vmem(2, 3, 2048), vmem(2, 4, 2048), vmem(2, 3, 2048), vmem(2, 4, 2048),
            *wave(5, 4), *wave(4, 4), *wave(3, 3),
            vmem(4, 2, 9, 4, 128), vmem(4, 2, 9, 4, 128), vmem(3, 2, 9, 4, 128),
            vmem(2, 9, 4, 128), vmem(9, 4, 128),
            sems(8), sems(4, 2), sems(2, 4), sems(2, 4), sems(2, 4, 3), sems(2, 3),
        ],
        compiler_params=pltpu.CompilerParams(collective_id=0, has_side_effects=True),
    )(*args)
    return start, grad_n, grad_k


def solution(mesh):
    space_n = mesh.shape["space"]

    def local(*args):
        return body(space_n, *args)

    return jax.shard_map(
        local,
        mesh=mesh,
        in_specs=(
            P("tm", None, "space", None),
            P("tm", None, "space", None),
            P("tm", None, None, "space", None),
            P("tm", None, None, "space", None),
            P("tm", "space", None),
            P("space", None),
            P("space", None),
            P(None, "space", None),
        ),
        out_specs=(P("tm", None, "space", None), P("space", "tm"), P(None, "space", "tm")),
        check_vma=False,
    )
```

```python
import jax
import jax.numpy as jnp
from jax import lax
from jax.experimental import pallas as pl
from jax.experimental.pallas import tpu as pltpu
from jax.sharding import PartitionSpec as P

TIME_STEP = 0.4
GRAVITY = 9.81
MESH = pl.DeviceIdType.MESH
F32 = jnp.float32


def remote(src, dst, send_sem, recv_sem, device):
    return pltpu.make_async_remote_copy(
        src_ref=src, dst_ref=dst, send_sem=send_sem, recv_sem=recv_sem,
        device_id=device, device_id_type=MESH,
    )


def kernel(
    space_n, end_hbm, depth_hbm, vel_hbm, salt_hbm, wet_hbm, cls_hbm, man_hbm, cond_hbm,
    out_ref, gn_ref, gk_ref,
    end_ref, depth_ref, vel_ref, salt_ref, wet_ref, cls_ref, man_ref, cond_ref,
    damp, hdamp, gcoef, source, fac_s, grads,
    down_out, up_out, down_in, up_in,
    off_0, core_0, pair_0, z_0, quad_0, y_0, back_0, home_0,
    off_1, core_1, pair_1, z_1, quad_1, y_1, back_1, home_1,
    off_f, core_f, pair_f, z_f, quad_f, y_f, back_f, home_f,
    core_g, sum_g, y_g, z_g_out, z_g,
    in_sems, halo_sems, core_sems, z_sems, y_sems, back_sems,
):
    sp = lax.axis_index("space")
    w = lax.axis_index("tm")
    core = lax.rem(w, 2)
    zh = lax.rem(lax.div(w, 2), 2)
    y = lax.div(w, 4)
    core_peer = (sp, w + 1 - 2 * core)
    z_peer = (sp, w + 2 - 4 * zh)
    has_prev = sp > 0
    has_next = sp < space_n - 1

    def y_peer(d):
        return (sp, lax.rem(w + 4 * d, 16))

    barrier = pltpu.get_barrier_semaphore()
    for peer in (z_peer, core_peer, y_peer(1), y_peer(2), y_peer(3)):
        pl.semaphore_signal(barrier, inc=1, device_id=peer, device_id_type=MESH)

    @pl.when(has_prev)
    def _():
        pl.semaphore_signal(barrier, inc=1, device_id=(sp - 1, w), device_id_type=MESH)

    @pl.when(has_next)
    def _():
        pl.semaphore_signal(barrier, inc=1, device_id=(sp + 1, w), device_id_type=MESH)

    loads = []
    for at, (src, dst) in enumerate((
        (end_hbm, end_ref), (depth_hbm, depth_ref), (vel_hbm, vel_ref), (salt_hbm, salt_ref),
        (wet_hbm, wet_ref), (cls_hbm, cls_ref), (man_hbm, man_ref), (cond_hbm, cond_ref),
    )):
        load = pltpu.make_async_copy(src, dst, in_sems.at[at])
        load.start()
        loads.append(load)

    last = jnp.where(w == 15, 1.0, 0.0).astype(F32)

    for d in (1, 2, 3):
        @pl.when(y + d > 3)
        def _(d=d):
            for slots in (y_0, y_1, y_f):
                slots[d - 1] = jnp.zeros(slots.shape[1:], F32)

    @pl.when(sp == 0)
    def _():
        down_in[...] = jnp.zeros(down_in.shape, F32)

    @pl.when(sp == space_n - 1)
    def _():
        up_in[...] = jnp.zeros(up_in.shape, F32)

    for load in loads:
        load.wait()

    def chunk(i, carry):
        block = lax.div(i, 4)
        g_core = lax.rem(i, 2)
        g_zh = lax.rem(lax.div(i, 2), 2)
        cols = pl.ds(pl.multiple_of(i * 128, 128), 128)
        sub = pl.ds(pl.multiple_of(lax.rem(i, 4) * 128, 128), 128)
        wet = wet_ref[0, :, cols].astype(F32)
        infil = TIME_STEP * wet * (0.25 + 0.75 * cls_ref[:, cols].astype(F32))
        man = man_ref[:, cols]
        cond = cond_ref[:, :, cols]
        mu = end_ref[0, 3:, :, cols]
        zero = jnp.zeros_like(mu[:1])
        cond_above = jnp.concatenate([zero, cond[:-1]], 0)
        factor = 1.0 / (1.0 + 4 * TIME_STEP * (cond + cond_above))
        gk = jnp.zeros_like(mu)
        start = mu
        for k in (3, 2, 1, 0):
            h = depth_ref[0, k, :, cols]
            u = vel_ref[0, k, 0, :, cols]
            v = vel_ref[0, k, 1, :, cols]
            speed = jnp.sqrt(u * u + v * v)
            powered = jnp.exp(4.0 / 3.0 * jnp.log(h))
            rate = GRAVITY * man * man * speed / powered
            relaxed = 1.0 + TIME_STEP * rate
            damping = wet / relaxed
            damp[k, :, cols] = damping
            hdamp[k, :, cols] = h * damping
            gcoef[k, :, cols] = (
                -2.0 * TIME_STEP * GRAVITY * man * speed * damping / (powered * relaxed)
            )
            if k == 0:
                off_0[block, 4, :, sub] = wet / (1.0 + 4 * TIME_STEP * rate)
            source[k, :, cols] = infil * mu[0]
            salt = salt_ref[0, k, :, :, cols].astype(F32)
            salt_below = jnp.concatenate([salt[1:], zero], 0)
            mu_below = jnp.concatenate([mu[1:], zero], 0)
            diff = mu_below - mu
            gk = gk - TIME_STEP * (salt_below - salt) * diff
            flux = cond * diff
            mu = mu + TIME_STEP * (flux - jnp.concatenate([zero, flux[:-1]], 0))
        held = factor * start
        offset = mu - held
        offset = offset + last * held
        off_0[block, 0:4, :, sub] = offset[0:4]
        off_1[block, :, :, sub] = offset[4:8]
        fac_s[block, :, :, sub] = factor
        grads[g_core, block, g_zh, 0:8] = gk
        return carry

    lax.fori_loop(0, 16, chunk, 0)

    pl.semaphore_wait(
        barrier, 5 + jnp.where(has_prev, 1, 0) + jnp.where(has_next, 1, 0)
    )

    other_half = pl.ds(2 * (1 - core), 2)
    waves = (
        (off_0, core_0, pair_0, z_0, quad_0, y_0, back_0, home_0),
        (off_1, core_1, pair_1, z_1, quad_1, y_1, back_1, home_1),
        (off_f, core_f, pair_f, z_f, quad_f, y_f, back_f, home_f),
    )
    core_copies = [
        remote(v[0].at[other_half], v[1], core_sems.at[0, i], core_sems.at[1, i], core_peer)
        for i, v in enumerate(waves)
    ]
    z_copies = [
        remote(v[4 if i == 1 else 2], v[3], z_sems.at[0, i], z_sems.at[1, i], z_peer)
        for i, v in enumerate(waves)
    ]
    y_copies = [
        [
            remote(v[2 if i == 1 else 4], v[5].at[d - 1], y_sems.at[0, i, d - 1], y_sems.at[1, i, d - 1],
                   y_peer(4 - d))
            for d in (1, 2, 3)
        ]
        for i, v in enumerate(waves)
    ]
    back_copies = [
        remote(v[6], v[7], back_sems.at[0, i], back_sems.at[1, i], core_peer)
        for i, v in enumerate(waves)
    ]

    def core_flow(b):
        mine = off_0[2 * core + b, 4]
        theirs = core_0[b, 4]
        return jnp.where(core == 0, mine, theirs), jnp.where(core == 0, theirs, mine)

    def z_flow(b):
        mine = pair_0[b, 4]
        theirs = z_0[b, 4]
        return jnp.where(zh == 0, mine, theirs), jnp.where(zh == 0, theirs, mine)

    def factors(i, b):
        return fac_s[2 * core + b, 4 * i : 4 * i + 4]

    def start_y(i):
        for d in (1, 2, 3):
            @pl.when(y >= d)
            def _(d=d):
                y_copies[i][d - 1].start()

    def wait_y(i):
        for d in (1, 2, 3):
            @pl.when(y + d <= 3)
            def _(d=d):
                y_copies[i][d - 1].wait_recv()

    def later_pairs(b):
        factor = factors(1, b)
        two = factor * factor
        four = two * two
        return y_1[0, b] + four * (y_1[1, b] + four * y_1[2, b]), two, four

    def z_of_wave_1():
        wait_y(1)
        for b in range(2):
            later, _, four = later_pairs(b)
            quad_1[b] = jnp.where(zh == 0, later, pair_1[b] + four * later)
        z_copies[1].start()

    def make_pair(i):
        off, arrived, pair = waves[i][:3]
        core_copies[i].wait_recv()
        for b in range(2):
            mine = off[2 * core + b]
            theirs = arrived[b]
            earlier = jnp.where(core == 0, mine, theirs)
            later = jnp.where(core == 0, theirs, mine)
            if i == 2:
                factor, _ = core_flow(b)
                pair[b, 0] = earlier[0] + later[0]
                pair[b, 1:3] = earlier[1:3] + factor[None] * later[1:3]
            else:
                pair[b, 0:4] = earlier[0:4] + factors(i, b) * later[0:4]
                if i == 0:
                    pair[b, 4] = earlier[4] * later[4]
        if i == 1:
            start_y(i)
        else:
            z_copies[i].start()

    def make_quad(i):
        pair, arrived, quad = waves[i][2:5]
        z_copies[i].wait_recv()
        for b in range(2):
            mine = pair[b]
            theirs = arrived[b]
            earlier = jnp.where(zh == 0, mine, theirs)
            later = jnp.where(zh == 0, theirs, mine)
            if i == 2:
                factor, _ = z_flow(b)
                quad[b, 0] = earlier[0] + later[0]
                quad[b, 1:3] = earlier[1:3] + factor[None] * later[1:3]
            else:
                factor = factors(i, b)
                quad[b, 0:4] = earlier[0:4] + factor * factor * later[0:4]
                if i == 0:
                    quad[b, 4] = earlier[4] * later[4]
        start_y(i)

    def results(i, block, offset, ends):
        cols = pl.ds(pl.multiple_of(block * 512, 512), 512)
        if i == 2:
            out_ref[0, 0, :, cols] = offset[0] + ends[0]
            out_ref[0, 1:3, :, cols] = offset[1:3] + off_0[block, 4][None] * ends[1:3]
        else:
            factor = fac_s[block, 4 * i : 4 * i + 4]
            out_ref[0, 3 + 4 * i : 7 + 4 * i, :, cols] = offset[0:4] + factor * ends

    def make_ends(i):
        off, arrived, pair, z_arrived, _, slots, back = waves[i][:7]
        if i == 1:
            z_copies[1].wait_recv()
        else:
            wait_y(i)
        own_ends = []
        for b in range(2):
            mine = off[2 * core + b]
            first = jnp.where(core == 0, arrived[b], mine)
            second = jnp.where(zh == 0, z_arrived[b], pair[b])
            if i == 2:
                _, core_factor = core_flow(b)
                _, z_factor = z_flow(b)

                def through(factor, map_, end):
                    return jnp.concatenate(
                        [map_[0:1] + end[0:1], map_[1:3] + factor[None] * end[1:3]], 0
                    )

                at_second = through(y_0[1, b, 4], slots[1, b], slots[2, b])
                at_second = through(y_0[0, b, 4], slots[0, b], at_second)
                at_first = through(z_factor, second, at_second)
                late = jnp.where(zh == 0, at_first, at_second)
                early = through(core_factor, first, late)
            elif i == 1:
                later, two, _ = later_pairs(b)
                late = z_1[b] + two * later
                early = first + factors(1, b) * late
            else:
                factor = factors(i, b)
                two = factor * factor
                four = two * two
                at_second = slots[0, b, 0:4] + four * (
                    slots[1, b, 0:4] + four * slots[2, b, 0:4]
                )
                at_first = second[0:4] + two * at_second
                late = jnp.where(zh == 0, at_first, at_second)
                early = first[0:4] + factor * late
            back[b] = jnp.where(core == 0, late, early)
            own_ends.append((mine, jnp.where(core == 0, early, late)))
        back_copies[i].start()
        for b, (mine, ends) in enumerate(own_ends):
            results(i, 2 * core + b, mine, ends)

    def finish(i):
        back_copies[i].wait_recv()
        for b in range(2):
            block = 2 * (1 - core) + b
            results(i, block, waves[i][0][block], waves[i][7][b])

    core_copies[0].start()
    core_copies[1].start()

    level = end_ref[0, 0]
    flow_x = end_ref[0, 1]
    flow_y = end_ref[0, 2]
    wet = wet_ref[0].astype(F32)
    n_cols = level.shape[1]
    grad_n = jnp.zeros_like(level)
    halo_copies = []

    def left(value):
        lanes = lax.broadcasted_iota(jnp.int32, value.shape, 1)
        return jnp.where(lanes == 0, 0.0, pltpu.roll(value, 1, 1))

    def right(value):
        lanes = lax.broadcasted_iota(jnp.int32, value.shape, 1)
        return jnp.where(lanes == n_cols - 1, 0.0, pltpu.roll(value, n_cols - 1, 1))

    def without_above(k, level, flow_x, flow_y):
        hdx = hdamp[k] * flow_x
        hdy = hdamp[k] * flow_y
        return hdx, level + TIME_STEP * hdx + TIME_STEP * (hdy - left(hdy))

    def advance(k, partial, hdx, above, below, flow_x, flow_y):
        mid = partial - TIME_STEP * jnp.concatenate([above, hdx[0:3]], 0)
        wet_mid = wet * mid
        after = jnp.concatenate([wet_mid[1:4], below], 0)
        damping = damp[k]
        return (
            mid + source[k],
            damping * flow_x + TIME_STEP * (after - wet_mid),
            damping * flow_y + TIME_STEP * (right(wet_mid) - wet_mid),
            wet_mid,
        )

    def friction_term(k, flow_x, flow_y):
        return gcoef[k] * (vel_ref[0, k, 0] * flow_x + vel_ref[0, k, 1] * flow_y)

    for turn, (k, k_next) in enumerate(((3, 2), (1, 0))):
        hdx, partial = without_above(k, level, flow_x, flow_y)
        first, second, third, fourth = (slice(r, r + 1) for r in range(4))
        wet_mid_3 = wet[fourth] * (partial[fourth] - TIME_STEP * hdx[third])
        held_x = damp[k] * flow_x
        hd_next = hdamp[k_next]
        down_out[turn, 0:1] = hdx[fourth]
        down_out[turn, 1:2] = hd_next[fourth] * (held_x[fourth] - TIME_STEP * wet_mid_3)
        down_out[turn, 2:3] = TIME_STEP * hd_next[fourth]
        wet_mid_0 = wet[first] * partial[first]
        wet_mid_1 = wet[second] * (partial[second] - TIME_STEP * hdx[first])
        row_x = held_x[first] + TIME_STEP * (wet_mid_1 - wet_mid_0)
        row_y = damp[k, 0:1] * flow_y[first] + TIME_STEP * (right(wet_mid_0) - wet_mid_0)
        row_hdy = hd_next[first] * row_y
        up_out[turn, 0:1] = wet_mid_0
        up_out[turn, 1:2] = wet[first]
        up_out[turn, 2:3] = (
            partial[first] + source[k, 0:1] + TIME_STEP * hd_next[first] * row_x
            + TIME_STEP * (row_hdy - left(row_hdy))
        )
        up_out[turn, 3:4] = hd_next[first]
        down = remote(
            down_out.at[turn], down_in.at[turn],
            halo_sems.at[0, turn], halo_sems.at[1, turn], (sp + 1, w),
        )
        up = remote(
            up_out.at[turn], up_in.at[turn],
            halo_sems.at[2, turn], halo_sems.at[3, turn], (sp - 1, w),
        )
        halo_copies.append((down, up))

        @pl.when(has_next)
        def _(down=down):
            down.start()

        @pl.when(has_prev)
        def _(up=up):
            up.start()

        if turn == 0:
            make_pair(0)
            make_pair(1)
        grad_n = grad_n + friction_term(k, flow_x, flow_y)

        @pl.when(has_prev)
        def _(down=down):
            down.wait_recv()

        @pl.when(has_next)
        def _(up=up):
            up.wait_recv()

        wet_4 = up_in[turn, 1:2]
        hd_4 = up_in[turn, 3:4]
        added = -TIME_STEP * hdx[fourth]
        wet_added = wet_4 * added
        added_y = hd_4 * (TIME_STEP * (right(wet_added) - wet_added))
        partial_4 = (
            up_in[turn, 2:3] + added - TIME_STEP * TIME_STEP * hd_4 * wet_added
            + TIME_STEP * (added_y - left(added_y))
        )
        level, flow_x, flow_y, wet_mid = advance(
            k, partial, hdx, down_in[turn, 0:1], up_in[turn, 0:1] + wet_added, flow_x, flow_y
        )
        grad_n = grad_n + friction_term(k_next, flow_x, flow_y)
        hdx, partial = without_above(k_next, level, flow_x, flow_y)
        above = down_in[turn, 1:2] + down_in[turn, 2:3] * wet_mid[first]
        below = wet_4 * (partial_4 - TIME_STEP * hdx[fourth])
        level, flow_x, flow_y, _ = advance(
            k_next, partial, hdx, above, below, flow_x, flow_y
        )

    for b in range(4):
        cols = slice(b * 512, b * 512 + 512)
        factor = off_0[b, 4]
        off_f[b, 0] = level[:, cols] - (1.0 - last) * end_ref[0, 0, :, cols]
        off_f[b, 1] = flow_x[:, cols] - (1.0 - last) * factor * end_ref[0, 1, :, cols]
        off_f[b, 2] = flow_y[:, cols] - (1.0 - last) * factor * end_ref[0, 2, :, cols]
    core_copies[2].start()
    for i in range(16):
        grads[i % 2, i // 4, i // 2 % 2, 8] = grad_n[:, i * 128 : i * 128 + 128]
    copy_core_g = remote(
        grads.at[1 - core], core_g, core_sems.at[0, 3], core_sems.at[1, 3], core_peer
    )
    copy_core_g.start()

    make_pair(2)
    z_of_wave_1()
    copy_core_g.wait_recv()
    sum_g[...] = grads[core] + core_g[...]
    copies_y_g = []
    for d in (1, 2, 3):
        copy = remote(
            sum_g.at[lax.rem(y + d, 4)], y_g.at[d - 1],
            y_sems.at[0, 3, d - 1], y_sems.at[1, 3, d - 1], y_peer(d),
        )
        copy.start()
        copies_y_g.append(copy)
    copy_z_g = remote(z_g_out.at[1 - zh], z_g, z_sems.at[0, 3], z_sems.at[1, 3], z_peer)

    make_quad(0)
    total = sum_g[y]
    for d in (1, 2, 3):
        copies_y_g[d - 1].wait_recv()
        total = total + y_g[d - 1]
    z_g_out[...] = total
    copy_z_g.start()
    make_ends(0)
    make_quad(2)
    finish(0)
    make_ends(1)
    make_ends(2)
    copy_z_g.wait_recv()
    total = z_g_out[zh] + z_g[...]
    gk_ref[...] = total[0:8]
    gn_ref[...] = total[8]
    finish(1)
    finish(2)

    for down, up in halo_copies:
        @pl.when(has_next)
        def _(down=down):
            down.wait_send()

        @pl.when(has_prev)
        def _(up=up):
            up.wait_send()

    for d in (1, 2, 3):
        @pl.when(y >= d)
        def _(d=d):
            for copies in y_copies:
                copies[d - 1].wait_send()

    for copy in core_copies + z_copies + back_copies + copies_y_g + [copy_core_g, copy_z_g]:
        copy.wait_send()


def hand_over(start_ref, grad_n_ref, grad_k_ref, start_out, grad_n_out, grad_k_out, sems):
    copies = []
    for at, (src, dst) in enumerate((
        (start_ref, start_out), (grad_n_ref, grad_n_out), (grad_k_ref, grad_k_out)
    )):
        copy = pltpu.make_async_copy(src, dst, sems.at[at])
        copy.start()
        copies.append(copy)
    for copy in copies:
        copy.wait()


def body(space_n, *args):
    def kern(*refs):
        kernel(space_n, *refs)

    def vmem(*shape):
        return pltpu.VMEM(shape, F32)

    def sems(*shape):
        return pltpu.SemaphoreType.DMA(shape)

    def wave(maps, ends):
        return [
            vmem(4, maps, 4, 512), vmem(2, maps, 4, 512), vmem(2, maps, 4, 512),
            vmem(2, maps, 4, 512), vmem(2, maps, 4, 512), vmem(3, 2, maps, 4, 512),
            vmem(2, ends, 4, 512), vmem(2, ends, 4, 512),
        ]

    start, grad_n, grad_k = pl.pallas_call(
        kern,
        out_shape=(
            jax.ShapeDtypeStruct((1, 11, 4, 2048), F32),
            jax.ShapeDtypeStruct((4, 128), F32),
            jax.ShapeDtypeStruct((8, 4, 128), F32),
        ),
        in_specs=[pl.BlockSpec(memory_space=pl.ANY)] * 8,
        out_specs=[pl.BlockSpec(memory_space=pltpu.VMEM)] * 3,
        scratch_shapes=[
            *[pltpu.VMEM(a.shape, a.dtype) for a in args],
            vmem(4, 4, 2048), vmem(4, 4, 2048), vmem(4, 4, 2048), vmem(4, 4, 2048),
            vmem(4, 8, 4, 512), vmem(2, 4, 2, 9, 4, 128),
            vmem(2, 3, 2048), vmem(2, 4, 2048), vmem(2, 3, 2048), vmem(2, 4, 2048),
            *wave(5, 4), *wave(4, 4), *wave(3, 3),
            vmem(4, 2, 9, 4, 128), vmem(4, 2, 9, 4, 128), vmem(3, 2, 9, 4, 128),
            vmem(2, 9, 4, 128), vmem(9, 4, 128),
            sems(8), sems(4, 2), sems(2, 4), sems(2, 4), sems(2, 4, 3), sems(2, 3),
        ],
        compiler_params=pltpu.CompilerParams(collective_id=0, has_side_effects=True),
    )(*args)
    return pl.pallas_call(
        hand_over,
        out_shape=tuple(jax.ShapeDtypeStruct(a.shape, a.dtype) for a in (start, grad_n, grad_k)),
        in_specs=[pl.BlockSpec(memory_space=pl.ANY)] * 3,
        out_specs=[pl.BlockSpec(memory_space=pltpu.VMEM)] * 3,
        scratch_shapes=[sems(3)],
    )(start, grad_n, grad_k)


def solution(mesh):
    space_n = mesh.shape["space"]

    def local(*args):
        return body(space_n, *args)

    return jax.shard_map(
        local,
        mesh=mesh,
        in_specs=(
            P("tm", None, "space", None),
            P("tm", None, "space", None),
            P("tm", None, None, "space", None),
            P("tm", None, None, "space", None),
            P("tm", "space", None),
            P("space", None),
            P("space", None),
            P(None, "space", None),
        ),
        out_specs=(P("tm", None, "space", None), P("space", "tm"), P(None, "space", "tm")),
        check_vma=False,
    )
```
